32 devices in a mesh: row: 8 (over z, core), col: 4 (over y, x).
Axes of the slice: x: 2, y: 2, z: 4, core: 2. Of those that a mesh axis runs over, the one named last changes fastest.
Arguments:
- roll_hidden: bfloat16 [1344, 4096], P(('row', 'col')), may hold values from -6 to 6
- roll_cotangent: bfloat16 [1344, 4096], P(('row', 'col')), may hold values from -6 to 6
- lengths: int32 [32], P(('row', 'col')), may hold values from 1 to 42, as said below
- owners: int32 [32], P(('row', 'col')), may hold values from 0 to 7, as said below
- prompts: int32 [32], P(('row', 'col')), may hold values from 0 to 3
- rewards: float32 [32], P(('row', 'col')), may hold values from -5 to 5
- gate_weight: bfloat16 [4096, 14784], P('col', 'row'), may hold values from -0.09375 to 0.09375
- up_weight: bfloat16 [4096, 14784], P('col', 'row'), may hold values from -0.09375 to 0.09375
- down_weight: bfloat16 [14784, 4096], P('row', 'col'), may hold values from -0.046875 to 0.046875
Outputs:
- grad_input: bfloat16 [1024, 4096], P('row', 'col')
- grad_gate: bfloat16 [4096, 14784], P('col', 'row')
- grad_up: bfloat16 [4096, 14784], P('col', 'row')
- grad_down: bfloat16 [14784, 4096], P('row', 'col')
The draws below stay inside these ranges and needn't reach their ends.
Inputs may be any that keep to these rules, and one draw needn't show every extreme that they name: `owners`: each owner value names exactly 4 rows; the lengths of one owner's rows sum to at most 128, and to exactly 128 for some owner in every draw. `lengths`: some row has length 42 in every draw.
All inputs are finite; a program needn't handle non-finite values.
Results may differ from the reference program's by a relative error of at most 0.025.
Values may be sent and summed in bfloat16 or wider, within the bound.
A program may use at most 128 MiB of HBM per device.

```python
import jax
import jax.numpy as jnp
from jax import lax

D = 4096
FF = 14784
CAPR = 128
MAXLEN = 42
OWNERS = 8
PER_OWNER = 4
ROWS = 32
PROMPTS = 4
TOKENS = 1024
N_COL = 4


def owner_table(key):
    key_perm = jax.random.fold_in(key, 101)
    key_special = jax.random.fold_in(key, 202)
    key_total = jax.random.fold_in(key, 303)
    key_share = jax.random.fold_in(key, 404)
    order = jax.random.permutation(key_perm, ROWS).astype(jnp.int32)
    owner = (order // PER_OWNER).astype(jnp.int32)
    place = (order % PER_OWNER).astype(jnp.int32)
    special = jax.random.randint(key_special, (), 0, OWNERS, dtype=jnp.int32)
    ids = jnp.arange(OWNERS, dtype=jnp.int32)
    total = jax.random.randint(key_total, (OWNERS,), CAPR // 2, CAPR + 1, dtype=jnp.int32)
    total = jnp.where(ids == special, CAPR, total)
    has_big = (ids == special).astype(jnp.int32)
    columns = jnp.arange(PER_OWNER, dtype=jnp.int32)
    is_big = (has_big[:, None] == 1) & (columns[None, :] == 0)
    shares = jax.random.randint(key_share, (OWNERS, PER_OWNER), 1, 4, dtype=jnp.int32)
    shares = jnp.where(has_big[:, None] == 1, 1, shares)
    shares = jnp.where(is_big, 0, shares)
    share_sum = jnp.sum(shares, 1)
    small_count = PER_OWNER - has_big
    extra = total - has_big * MAXLEN - small_count
    portion = extra[:, None] * shares // share_sum[:, None]
    remain = extra - jnp.sum(portion, 1)
    ranks = columns[None, :] - has_big[:, None]
    bump = ((ranks < remain[:, None]) & jnp.logical_not(is_big)).astype(jnp.int32)
    raw = jnp.minimum(1 + portion + bump, MAXLEN)
    parts = jnp.where(is_big, MAXLEN, raw).astype(jnp.int32)
    lengths = parts[owner, place].astype(jnp.int32)
    return (lengths, owner)


def draw_lengths(key, part):
    return owner_table(key)[0]


def draw_owners(key, part):
    return owner_table(key)[1]


def place_ends(entries, key, least, largest):
    longest = entries.shape.index(max(entries.shape))
    spots = []
    for shift in (0, 1):
        where = [jax.random.randint(jax.random.fold_in(key, axis), (), 0, length) for axis, length in enumerate(entries.shape)]
        where[longest] = (where[longest] + shift) % entries.shape[longest]
        spots.append(tuple(where))
    return entries.at[spots[0]].set(least).at[spots[1]].set(largest)


def block_scale(stream_key, dims, split, smallest, top_value):
    gain, own = 1.0, jax.random.fold_in(stream_key, 6)
    for axis_at, blocks in split:
        draws = jnp.exp(jax.random.uniform(jax.random.fold_in(own, axis_at), (blocks,), jnp.float32, smallest / len(split), top_value / len(split)))
        gain = gain * jnp.repeat(draws, dims[axis_at] // blocks).reshape([-1 if axis == axis_at else 1 for axis in range(len(dims))])
    return gain


def normal_values(key, shape, deviation, most, pieces=(), kind=jnp.bfloat16):
    values = deviation * jax.random.normal(key, shape, jnp.float32)
    if pieces:
        values = values * block_scale(key, shape, pieces, -0.22, 0.18)
    return jnp.clip(values, -most, most).astype(kind)


def setup_inputs(seed: int = 0) -> dict:
    streams_of = jax.random.split(jax.random.key(seed), 10)
    roll_hidden = normal_values(streams_of[0], (ROWS * MAXLEN, D), 1.0, 6.0, ((0, 32),))
    roll_cotangent = normal_values(streams_of[1], (ROWS * MAXLEN, D), 1.0, 6.0, ((0, 32),))
    lengths = draw_lengths(jax.random.fold_in(streams_of[9], 71), 0)
    owners = draw_owners(jax.random.fold_in(streams_of[9], 71), 0)
    prompts = place_ends(jax.random.randint(streams_of[4], (ROWS,), 0, PROMPTS), jax.random.fold_in(streams_of[4], 1), 0, PROMPTS - 1).astype(jnp.int32)
    rewards = normal_values(streams_of[5], (ROWS,), 1.0, 5.0, ((0, 32),), jnp.float32)
    gate_weight = normal_values(streams_of[6], (D, FF), D ** -0.5, 0.09375, ((0, 4), (1, 8)))
    up_weight = normal_values(streams_of[7], (D, FF), D ** -0.5, 0.09375, ((0, 4), (1, 8)))
    down_weight = normal_values(streams_of[8], (FF, D), FF ** -0.5, 0.046875, ((0, 8), (1, 4)))
    return {"roll_hidden": roll_hidden, "roll_cotangent": roll_cotangent, "lengths": lengths, "owners": owners, "prompts": prompts, "rewards": rewards, "gate_weight": gate_weight, "up_weight": up_weight, "down_weight": down_weight}


spread_floor = 0.7

def row_weights(lengths, prompts, rewards, count_prompts):
    onehot = (prompts[:, None] == jnp.arange(count_prompts, dtype=jnp.int32)[None, :]).astype(jnp.float32)
    counts = jnp.maximum(lax.optimization_barrier(jnp.sum(onehot, 0)), 1.0)
    means = lax.optimization_barrier(jnp.sum(onehot * rewards[:, None], 0)) / counts
    centred = rewards - lax.optimization_barrier(jnp.sum(onehot * means[None, :], 1))
    spreads = jnp.sqrt(lax.optimization_barrier(jnp.sum(onehot * (centred * centred)[:, None], 0)) / counts)
    divisor = jnp.maximum(lax.optimization_barrier(jnp.sum(onehot * spreads[None, :], 1)), spread_floor)
    return centred / divisor / lengths.astype(jnp.float32)

def row_offsets(lengths, owners):
    count = lengths.shape[0]
    places = jnp.arange(count, dtype=jnp.int32)
    earlier = (owners[None, :] == owners[:, None]) & (places[None, :] < places[:, None])
    return lax.optimization_barrier(jnp.sum(jnp.where(earlier, lengths[None, :], 0), 1)).astype(jnp.int32)

def block_sum(left, right, blocks, transpose_right):
    width = left.shape[1] // blocks
    total = None
    for index in range(blocks):
        piece = left[:, index * width:(index + 1) * width]
        if transpose_right:
            other = right[:, index * width:(index + 1) * width]
            term = lax.dot_general(piece, other, (((1,), (1,)), ((), ())), preferred_element_type=jnp.float32)
        else:
            other = right[index * width:(index + 1) * width, :]
            term = jnp.dot(piece, other, preferred_element_type=jnp.float32)
        term = lax.optimization_barrier(term.astype(jnp.bfloat16)).astype(jnp.float32)
        total = term if total is None else total + term
    return total

def reference(roll_hidden, roll_cotangent, lengths, owners, prompts, rewards, gate_weight, up_weight, down_weight):
    weight = row_weights(lengths, prompts, rewards, PROMPTS)
    offsets = row_offsets(lengths, owners)
    slots = jnp.arange(MAXLEN, dtype=jnp.int32)
    live = slots[None, :] < lengths[:, None]
    target = jnp.where(live, owners[:, None] * CAPR + offsets[:, None] + slots[None, :], TOKENS).astype(jnp.int32)
    hidden_rows = roll_hidden.reshape(ROWS, MAXLEN, D)
    cot_rows = roll_cotangent.reshape(ROWS, MAXLEN, D).astype(jnp.float32)
    upstream = jnp.where(live[:, :, None], cot_rows * weight[:, None, None], 0.0).astype(jnp.bfloat16)
    flat_target = target.reshape(-1)
    packed = jnp.zeros((TOKENS, D), jnp.bfloat16).at[flat_target].set(hidden_rows.reshape(-1, D), mode='drop')
    packed_grad = jnp.zeros((TOKENS, D), jnp.bfloat16).at[flat_target].set(upstream.reshape(-1, D), mode='drop')
    gate = block_sum(packed, gate_weight, N_COL, False)
    upval = block_sum(packed, up_weight, N_COL, False)
    sig = jax.nn.sigmoid(gate)
    silu = gate * sig
    hidden = (silu * upval).astype(jnp.bfloat16)
    grad_hidden = block_sum(packed_grad, down_weight, N_COL, True)
    grad_gate_act = (grad_hidden * upval * sig * (1.0 + gate * (1.0 - sig))).astype(jnp.bfloat16)
    grad_up_act = (grad_hidden * silu).astype(jnp.bfloat16)
    contract_rows = (((0,), (0,)), ((), ()))
    grad_down = lax.dot_general(hidden, packed_grad, contract_rows, preferred_element_type=jnp.float32).astype(jnp.bfloat16)
    grad_gate = lax.dot_general(packed, grad_gate_act, contract_rows, preferred_element_type=jnp.float32).astype(jnp.bfloat16)
    grad_up = lax.dot_general(packed, grad_up_act, contract_rows, preferred_element_type=jnp.float32).astype(jnp.bfloat16)
    contract_cols = (((1,), (1,)), ((), ()))
    grad_input = lax.dot_general(grad_gate_act, gate_weight, contract_cols, preferred_element_type=jnp.float32)
    grad_input = grad_input + lax.dot_general(grad_up_act, up_weight, contract_cols, preferred_element_type=jnp.float32)
    return (grad_input.astype(jnp.bfloat16), grad_gate, grad_up, grad_down)
```

```python
import functools

import jax
import jax.numpy as jnp
from jax import lax
from jax.experimental import pallas as pl
from jax.experimental.pallas import tpu as pltpu
from jax.sharding import PartitionSpec as P

CAPR = 128
MESH = pl.DeviceIdType.MESH
SIZES = (12, 13, 14)


spread_floor = 0.7


def row_weights(lengths, prompts, rewards, count_prompts):
    onehot = (prompts[:, None] == jnp.arange(count_prompts, dtype=jnp.int32)[None, :]).astype(
        jnp.float32
    )
    counts = jnp.maximum(jnp.sum(onehot, 0), 1.0)
    means = jnp.sum(onehot * rewards[:, None], 0) / counts
    centred = rewards - jnp.sum(onehot * means[None, :], 1)
    spreads = jnp.sqrt(jnp.sum(onehot * (centred * centred)[:, None], 0) / counts)
    divisor = jnp.maximum(jnp.sum(onehot * spreads[None, :], 1), spread_floor)
    return centred / divisor / lengths.astype(jnp.float32)


def row_offsets(lengths, owners):
    count = lengths.shape[0]
    places = jnp.arange(count, dtype=jnp.int32)
    earlier = (owners[None, :] == owners[:, None]) & (places[None, :] < places[:, None])
    return jnp.sum(jnp.where(earlier, lengths[None, :], 0), 1)


def table_kernel(mine_ref, all_ref, send_sem, recv_sem, own_sem):
    row, col = lax.axis_index("row"), lax.axis_index("col")
    row_count, col_count = lax.axis_size("row"), lax.axis_size("col")
    barrier = pltpu.get_barrier_semaphore()

    def col_peer(step):
        return (row, lax.rem(col + step, col_count))

    def row_peer(step):
        return (lax.rem(row + step, row_count), col)

    for step in range(1, col_count):
        pl.semaphore_signal(barrier, inc=1, device_id=col_peer(step), device_id_type=MESH)
    for step in range(1, row_count):
        pl.semaphore_signal(barrier, inc=1, device_id=row_peer(step), device_id_type=MESH)
    own = pltpu.make_async_copy(mine_ref, all_ref.at[row * col_count + col], own_sem)
    own.start()
    pl.semaphore_wait(barrier, col_count + row_count - 2)
    copies = [
        pltpu.make_async_remote_copy(
            src_ref=mine_ref,
            dst_ref=all_ref.at[row * col_count + col],
            send_sem=send_sem.at[step],
            recv_sem=recv_sem.at[step],
            device_id=col_peer(step),
            device_id_type=MESH,
        )
        for step in range(1, col_count)
    ]
    for copy in copies:
        copy.start()
    own.wait()
    for copy in copies:
        copy.wait_recv()
    held = all_ref.at[pl.ds(row * col_count, col_count)]
    onward = [
        pltpu.make_async_remote_copy(
            src_ref=held,
            dst_ref=held,
            send_sem=send_sem.at[col_count + step],
            recv_sem=recv_sem.at[col_count + step],
            device_id=row_peer(step),
            device_id_type=MESH,
        )
        for step in range(1, row_count)
    ]
    for copy in onward:
        copy.start()
    for copy in onward:
        copy.wait_recv()
    for copy in copies + onward:
        copy.wait_send()


def gather_table(local):
    row_count, col_count = lax.axis_size("row"), lax.axis_size("col")
    devices = row_count * col_count
    mine = jnp.pad(local, ((0, 0), (0, 128 - local.shape[1])))
    every = pl.pallas_call(
        table_kernel,
        out_shape=jax.ShapeDtypeStruct((devices, 1, 128), jnp.float32),
        in_specs=[pl.BlockSpec(memory_space=pltpu.VMEM)],
        out_specs=pl.BlockSpec(memory_space=pltpu.VMEM),
        scratch_shapes=[
            pltpu.SemaphoreType.DMA((row_count + col_count,)),
            pltpu.SemaphoreType.DMA((row_count + col_count,)),
            pltpu.SemaphoreType.DMA,
        ],
        compiler_params=pltpu.CompilerParams(collective_id=2, has_side_effects=True),
    )(mine)
    return every[:, 0, : local.shape[1]]


UNIT = 384


def padded_slots(slots):
    return -(-slots // 16) * 16


class Line:
    def __init__(self, every, size, send_sem, recv_sem, pieces):
        self.every, self.send_sem, self.recv_sem, self.pieces = every, send_sem, recv_sem, pieces
        self.size = size
        row, self.col = lax.axis_index("row"), lax.axis_index("col")
        self.chips = lax.axis_size("row") // 2
        self.core, self.chip = lax.rem(row, 2), lax.div(row, 2)

    def place(self, r, c):
        first = pl.multiple_of((r * self.pieces + c) * self.size, self.size)
        return self.every.at[pl.ds(first, self.size)]

    def hop(self, way, r, c):
        index = (r, c) if self.pieces > 1 else (r,)
        target = (
            (self.chip + 1) * 2 + self.core,
            (self.chip - 1) * 2 + self.core,
            self.chip * 2 + 1 - self.core,
        )[way]
        place = self.place(r, c)
        return pltpu.make_async_remote_copy(
            src_ref=place,
            dst_ref=place,
            send_sem=self.send_sem.at[(way,) + index],
            recv_sem=self.recv_sem.at[index],
            device_id=(target, self.col),
            device_id_type=MESH,
        )

    def has(self, way):
        return (self.chip + 1 < self.chips, self.chip > 0)[way]

    def offer(self, r, c):
        for way in range(2):
            pl.when(self.has(way))(lambda: self.hop(way, r, c).start())
        self.hop(2, r, c).start()

    def there(self, d, side):
        source = self.chip + d if side else self.chip - d
        return source, (source < self.chips) if side else (source >= 0)

    def pass_on(self, d):
        for c in range(self.pieces):
            for side in range(2):
                source, valid = self.there(d, side)
                r = source * 2 + self.core

                @pl.when(valid)
                def _():
                    self.hop(2, r, c).wait_recv()
                    pl.when(self.has(side))(lambda: self.hop(side, r, c).start())
                    self.hop(2, r, c).start()

    def partner(self, source):
        for c in range(self.pieces):
            self.hop(2, source * 2 + 1 - self.core, c).wait_recv()

    def sent(self):
        def chip_sent(source, carry):
            r = source * 2 + self.core
            for c in range(self.pieces):

                @pl.when((source <= self.chip) & (self.chip + 1 < self.chips))
                def _():
                    self.hop(0, r, c).wait_send()

                @pl.when((source >= self.chip) & (self.chip > 0))
                def _():
                    self.hop(1, r, c).wait_send()

                self.hop(2, r, c).wait_send()
            return carry

        lax.fori_loop(0, self.chips, chip_sent, 0)


def gather_kernel(
    mine_ref,
    hidden_ref,
    cotangent_ref,
    table_ref,
    packed_ref,
    cot_ref,
    target_ref,
    hidden_mine,
    cot_mine,
    every,
    acc,
    table_sems,
    own_sem,
    cols_sems,
    line_send,
    line_recv,
):
    row, col = lax.axis_index("row"), lax.axis_index("col")
    row_count, col_count = lax.axis_size("row"), lax.axis_size("col")
    slots = hidden_ref.shape[0]
    pad, width = hidden_mine.shape[1:]
    line = Line(every, pad, line_send, line_recv, col_count)

    def col_peer(step):
        return (row, lax.rem(col + step, col_count))

    def row_peer(step):
        return (lax.rem(row + step, row_count), col)

    barrier = pltpu.get_barrier_semaphore()
    for step in range(1, col_count):
        pl.semaphore_signal(barrier, inc=1, device_id=col_peer(step), device_id_type=MESH)
    for step in range(1, row_count):
        pl.semaphore_signal(barrier, inc=1, device_id=row_peer(step), device_id_type=MESH)
    own = pltpu.make_async_copy(mine_ref, table_ref.at[row * col_count + col], own_sem)
    own.start()
    for source, held in ((hidden_ref, hidden_mine), (cotangent_ref, cot_mine)):
        for c in range(col_count):
            if pad > slots:
                held[c, pl.ds(pad - 16, 16), :] = jnp.zeros((16, width), held.dtype)
            held[c, pl.ds(0, slots), :] = source[:, pl.ds(c * width, width)]
    mine_at = pl.multiple_of((row * col_count + col) * pad, pad)
    cot_at = pl.multiple_of(col * pad, pad)
    every[pl.ds(mine_at, pad), :] = hidden_mine[col]
    cot_ref[pl.ds(cot_at, pad), :] = cot_mine[col]
    pl.semaphore_wait(barrier, col_count + row_count - 2)

    def table_copy(kind, step, place, target):
        return pltpu.make_async_remote_copy(
            src_ref=place,
            dst_ref=place,
            send_sem=table_sems.at[0, kind, step],
            recv_sem=table_sems.at[1, kind, step],
            device_id=target,
            device_id_type=MESH,
        )

    def cols_copy(kind, step):
        held = (hidden_mine, cot_mine)[kind]
        place = every.at[pl.ds(mine_at, pad)] if kind == 0 else cot_ref.at[pl.ds(cot_at, pad)]
        return pltpu.make_async_remote_copy(
            src_ref=held.at[lax.rem(col + step, col_count)],
            dst_ref=place,
            send_sem=cols_sems.at[kind, 0, step],
            recv_sem=line_recv.at[row, col] if kind == 0 else cols_sems.at[kind, 1, step],
            device_id=col_peer(step),
            device_id_type=MESH,
        )

    own.wait()
    table_cols = [
        table_copy(0, step, table_ref.at[row * col_count + col], col_peer(step))
        for step in range(1, col_count)
    ]
    for move in table_cols:
        move.start()
    hidden_cols = [cols_copy(0, step) for step in range(1, col_count)]
    cot_cols = [cols_copy(1, step) for step in range(1, col_count)]
    for move in hidden_cols:
        move.start()
    line.offer(row, col)
    for move in cot_cols:
        move.start()
    for move in table_cols:
        move.wait_recv()
    held_rows = table_ref.at[pl.ds(row * col_count, col_count)]
    table_rows = [
        table_copy(1, step, held_rows, row_peer(step)) for step in range(1, row_count)
    ]
    for move in table_rows:
        move.start()
    for step in range(1, col_count):
        c = lax.rem(col + step, col_count)
        line.hop(2, row, c).wait_recv()
        line.offer(row, c)
    for move in table_rows:
        move.wait_recv()

    count = row_count * col_count
    lengths = table_ref[...].reshape(count, 128)[:, 0:1]
    across = lax.broadcasted_iota(jnp.int32, (count, count), 1)
    below = lax.broadcasted_iota(jnp.int32, (count, count), 0)
    as_row = jnp.sum(jnp.where(across == below, lengths, 0.0), 0, keepdims=True)
    starts = jnp.sum(jnp.where(across < below, as_row, 0.0), 1, keepdims=True)
    lanes = lax.broadcasted_iota(jnp.int32, (count, count * pad), 1)
    rows = lax.broadcasted_iota(jnp.int32, (count, count * pad), 0)
    spot = (lanes - rows * pad).astype(jnp.float32)
    live = (spot >= 0.0) & (spot < lengths)
    spots = jnp.sum(jnp.where(live, starts + spot + 1.0, 0.0), 0, keepdims=True) - 1.0
    target_ref[...] = spots.astype(jnp.int32)

    acc[...] = jnp.zeros_like(acc)
    chip_rows = 2 * col_count * pad
    tokens = packed_ref.shape[0]
    half = tokens // 4

    def gathered(d, carry):
        @pl.when(d > 0)
        def _():
            line.pass_on(d)

        def take(side, c):
            source = line.chip + jnp.where(side == 1, d, -d)
            valid = (source >= 0) & (source < line.chips) & ((d > 0) | (side == 0))

            @pl.when(valid)
            def _():
                line.partner(source)
                where = pl.ds(pl.multiple_of(source * chip_rows, 128), chip_rows)
                wanted = target_ref[:, where]
                block = every[where, :]

                def part(n, c):
                    place = pl.ds(pl.multiple_of(n * half, half), half)
                    ids = lax.broadcasted_iota(jnp.int32, (half, chip_rows), 0) + n * half
                    pick = (ids == wanted).astype(jnp.bfloat16)
                    acc[place, :] += jnp.dot(pick, block, preferred_element_type=jnp.float32)
                    return c

                lax.fori_loop(0, 4, part, 0)

            return c

        return lax.fori_loop(0, 2, take, carry)

    lax.fori_loop(0, line.chips, gathered, 0)
    packed_ref[...] = acc[...].astype(packed_ref.dtype)
    for move in cot_cols:
        move.wait_recv()
    for move in table_cols + table_rows + hidden_cols + cot_cols:
        move.wait_send()
    line.sent()


def gather_rows(local, roll_hidden, roll_cotangent, total_tokens):
    row_count, col_count = lax.axis_size("row"), lax.axis_size("col")
    devices = row_count * col_count
    slots, whole = roll_hidden.shape
    width = whole // col_count
    pad = padded_slots(slots)
    low = roll_hidden.dtype
    mine = jnp.pad(local, ((0, 0), (0, 128 - local.shape[1])))
    vmem = pl.BlockSpec(memory_space=pltpu.VMEM)
    steps = max(row_count, col_count)
    return pl.pallas_call(
        gather_kernel,
        out_shape=[
            jax.ShapeDtypeStruct((devices, 1, 128), jnp.float32),
            jax.ShapeDtypeStruct((total_tokens, width), low),
            jax.ShapeDtypeStruct((col_count * pad, width), low),
            jax.ShapeDtypeStruct((1, devices * pad), jnp.int32),
        ],
        in_specs=[vmem] * 3,
        out_specs=[vmem] * 4,
        scratch_shapes=[
            pltpu.VMEM((col_count, pad, width), low),
            pltpu.VMEM((col_count, pad, width), low),
            pltpu.VMEM((row_count * col_count * pad, width), low),
            pltpu.VMEM((total_tokens, width), jnp.float32),
            pltpu.SemaphoreType.DMA((2, 2, steps)),
            pltpu.SemaphoreType.DMA,
            pltpu.SemaphoreType.DMA((2, 2, col_count)),
            pltpu.SemaphoreType.DMA((3, row_count, col_count)),
            pltpu.SemaphoreType.DMA((row_count, col_count)),
        ],
        compiler_params=pltpu.CompilerParams(
            collective_id=2, has_side_effects=True, vmem_limit_bytes=48 * 1024 * 1024
        ),
    )(mine, roll_hidden, roll_cotangent)


def fused_kernel(
    dims,
    pk_ref,
    cot_ref,
    weight_ref,
    target_ref,
    held_ref,
    gw_ref,
    uw_ref,
    dw_ref,
    gi_ref,
    gg_ref,
    gu_ref,
    gd_ref,
    weights,
    tokens_held,
    every,
    parts,
    first_in,
    second_in,
    results,
    acc,
    spread,
    pair_in,
    chip_in,
    send_sem,
    recv_sem,
    weight_sem,
    held_sem,
    line_send,
    line_recv,
    out_sem,
    pair_sem,
    chip_sem,
):
    tokens, units, blocks = dims
    quarter = tokens // 4
    row, col = lax.axis_index("row"), lax.axis_index("col")
    row_count, col_count = lax.axis_size("row"), lax.axis_size("col")
    chips = row_count // 2
    x, y = lax.rem(col, 2), lax.div(col, 2)
    core, chip = lax.rem(row, 2), lax.div(row, 2)
    x_peer, y_peer = y * 2 + (1 - x), (1 - y) * 2 + x
    other_core = chip * 2 + 1 - core
    last = units - (blocks - 1) * UNIT
    slots = held_ref.shape[1]
    width = cot_ref.shape[1]
    pad = cot_ref.shape[0] // col_count
    line = Line(every, col_count * pad, line_send, line_recv, 1)

    def load(i, j, size):
        place = pl.ds(j * UNIT, size)
        return pltpu.make_async_copy(
            (gw_ref, uw_ref, dw_ref)[i].at[place], weights.at[i, place], weight_sem.at[i, j]
        )

    def block_size(j):
        return UNIT if j < blocks - 1 else last

    bring = pltpu.make_async_copy(
        pk_ref.at[pl.ds(0, tokens)], tokens_held.at[0], held_sem.at[0]
    )
    bring_cot = pltpu.make_async_copy(cot_ref, line.place(row, 0), held_sem.at[1])
    bring.start()
    for j in range(blocks):
        for i in range(2):
            load(i, j, block_size(j)).start()
        if j == 0:
            bring_cot.start()
    for j in range(blocks):
        load(2, j, block_size(j)).start()

    def chip_peer(step):
        return lax.rem(chip + step, chips) * 2 + core

    barrier = pltpu.get_barrier_semaphore()
    for peer in (x_peer, y_peer):
        pl.semaphore_signal(barrier, inc=1, device_id=(row, peer), device_id_type=MESH)
    pl.semaphore_signal(barrier, inc=1, device_id=(other_core, col), device_id_type=MESH)
    for step in range(1, chips):
        pl.semaphore_signal(
            barrier, inc=1, device_id=(chip_peer(step), col), device_id_type=MESH
        )
    if blocks * UNIT > units:
        for i in range(3):
            weights[i, pl.ds(units, blocks * UNIT - units), :] = jnp.zeros(
                (blocks * UNIT - units, width), weights.dtype
            )
    pl.semaphore_wait(barrier, 2 + chips)

    def copy(step, i, j, way):
        if step == 0:
            src = parts.at[i, j, 1 - x] if way == 0 else parts.at[i, j, :, 1 - y]
            dst = first_in.at[i, j]
        elif step == 1:
            src = parts.at[i, j, x, 1 - y] if way == 0 else parts.at[i, j, 1 - x, y]
            dst = second_in.at[i, j]
        elif step == 2:
            src = dst = results.at[i, j, x, y]
        else:
            src = dst = results.at[i, j, x] if way == 0 else results.at[i, j, :, y]
        along_x = (way == 0) == (step in (0, 3))
        return pltpu.make_async_remote_copy(
            src_ref=src,
            dst_ref=dst,
            send_sem=send_sem.at[step, i, j],
            recv_sem=recv_sem.at[step, i, j],
            device_id=(row, x_peer if along_x else y_peer),
            device_id_type=MESH,
        )

    def each_way(i, j, act):
        if isinstance(i, int) and i < 2:
            act(i)
        else:
            chosen = i if not isinstance(i, int) else lax.rem(j, 2)
            for way in range(2):
                pl.when(chosen == way)(functools.partial(act, way))

    def start(step, i, j):
        each_way(i, j, lambda way: copy(step, i, j, way).start())

    def arrive(step, i, j):
        each_way(i, j, lambda way: copy(step, i, j, way).wait_recv())

    def block_rows(j):
        return pl.ds(pl.multiple_of(j * UNIT, 128), UNIT)

    def half_rows(a):
        return pl.ds(pl.multiple_of(a * 2 * quarter, 2 * quarter), 2 * quarter)

    across = (((1,), (1,)), ((), ()))
    plain = (((1,), (0,)), ((), ()))
    down = (((0,), (0,)), ((), ()))

    def loaded(i, j):
        for which in range(3):

            @pl.when((i == which) & (j < blocks - 1))
            def _():
                load(which, j, UNIT).wait()

            @pl.when((i == which) & (j == blocks - 1))
            def _():
                load(which, j, last).wait()

    def forward(i, j, which):
        loaded(i, j)

        def part(a, c):
            term = lax.dot_general(
                tokens_held[which, half_rows(a), :],
                weights[i, block_rows(j), :],
                across,
                preferred_element_type=jnp.float32,
            )
            parts[i, j, a] = term.astype(jnp.bfloat16).reshape(2, quarter, UNIT)
            return c

        lax.fori_loop(0, 2, part, 0)
        start(0, i, j)

    def halve(i, j):
        def act(way):
            copy(0, i, j, way).wait_recv()
            if way == 0:
                total = parts[i, j, x, 1 - y].astype(jnp.float32)
                total = total + first_in[i, j, 1 - y].astype(jnp.float32)
                parts[i, j, x, 1 - y] = total.astype(jnp.bfloat16)
            else:
                total = parts[i, j, 1 - x, y].astype(jnp.float32)
                total = total + first_in[i, j, 1 - x].astype(jnp.float32)
                parts[i, j, 1 - x, y] = total.astype(jnp.bfloat16)
            copy(1, i, j, way).start()

        each_way(i, j, act)

    def own_sum(i, j):
        arrive(1, i, j)
        place = (y, x)[i] if i < 2 else lax.rem(j, 2) * x + (1 - lax.rem(j, 2)) * y
        return (
            parts[i, j, x, y].astype(jnp.float32)
            + first_in[i, j, place].astype(jnp.float32)
            + second_in[i, j].astype(jnp.float32)
        )

    bring.wait()
    bring_cot.wait()

    def phase_up(n, carry):
        forward(lax.rem(n, 2), lax.div(n, 2), 0)

        @pl.when(n == 0)
        def _():
            line.offer(row, 0)

        return carry

    lax.fori_loop(0, 2 * blocks, phase_up, 0)
    acc[...] = jnp.zeros_like(acc)

    def phase_up_halve(j, carry):
        @pl.when((j >= 1) & (j < chips))
        def _():
            line.pass_on(j)

        halve(0, j)
        halve(1, j)
        return carry

    def some_halves(first, end):
        lax.fori_loop(first, end, phase_up_halve, 0)

    early = min(chips, blocks)
    some_halves(0, early)
    for d in range(early, chips):
        line.pass_on(d)

    def partners(source, carry):
        line.partner(source)
        return carry

    lax.fori_loop(0, chips, partners, 0)
    line.sent()

    def scale(k, carry):
        where = pl.ds(pl.multiple_of(k * pad, pad), pad)
        scaled = every[where, :].astype(jnp.float32) * weight_ref[k]
        every[where, :] = scaled.astype(jnp.bfloat16)
        return carry

    lax.fori_loop(0, row_count * col_count, scale, 0)

    def pick(n, carry):
        place = pl.ds(pl.multiple_of(n * quarter, quarter), quarter)
        ids = lax.broadcasted_iota(jnp.int32, (quarter, target_ref.shape[1]), 0) + n * quarter
        tokens_held[1, place, :] = jnp.dot(
            (ids == target_ref[...]).astype(jnp.bfloat16),
            every[pl.ds(0, target_ref.shape[1]), :],
            preferred_element_type=jnp.float32,
        ).astype(jnp.bfloat16)
        return carry

    lax.fori_loop(0, 4, pick, 0)

    def phase_down(j, carry):
        forward(2, j, 1)
        return carry

    lax.fori_loop(0, blocks, phase_down, 0)
    some_halves(early, blocks)

    def phase_down_halve(j, carry):
        halve(2, j)
        return carry

    lax.fori_loop(0, blocks, phase_down_halve, 0)

    def phase_own(j, carry):
        gate, upval, grad_hidden = (own_sum(i, j) for i in range(3))
        sig = jax.nn.sigmoid(gate)
        silu = gate * sig
        results[2, j, x, y] = (silu * upval).astype(jnp.bfloat16)
        results[0, j, x, y] = (grad_hidden * upval * sig * (1.0 + gate * (1.0 - sig))).astype(
            jnp.bfloat16
        )
        results[1, j, x, y] = (grad_hidden * silu).astype(jnp.bfloat16)
        start(2, 0, j)
        start(2, 1, j)

        @pl.when(j > 0)
        def _():
            for i in range(2):
                arrive(2, i, j - 1)
                start(3, i, j - 1)

        return carry

    lax.fori_loop(0, blocks, phase_own, 0)
    for i in range(2):
        arrive(2, i, blocks - 1)
        start(3, i, blocks - 1)

    def phase_share(j, carry):
        start(2, 2, j)
        return carry

    lax.fori_loop(0, blocks, phase_share, 0)

    def staged(slot, j, size):
        return pl.ds(pl.multiple_of((slot * 2 + lax.rem(j, 2)) * UNIT, UNIT), size)

    def out_copy(which, i, j, size):
        return pltpu.make_async_copy(
            every.at[staged(i, j, size)],
            (gg_ref, gu_ref, gd_ref)[which].at[pl.ds(pl.multiple_of(j * UNIT, 128), size)],
            out_sem.at[i, lax.rem(j, 2)],
        )

    def emit(i, j, which, slot, held):
        @pl.when(j > 1)
        def _():
            out_copy(0, slot, j - 2, UNIT).wait()

        every[staged(slot, j, UNIT), :] = lax.dot_general(
            results[i, j].reshape(tokens, UNIT),
            tokens_held[held],
            down,
            preferred_element_type=jnp.float32,
        ).astype(jnp.bfloat16)
        for kind in which:

            @pl.when((i == kind) & (j < blocks - 1))
            def _():
                out_copy(kind, slot, j, UNIT).start()

            @pl.when((i == kind) & (j == blocks - 1))
            def _():
                out_copy(kind, slot, j, last).start()

    def drain(kind, slot):
        if blocks > 1:
            out_copy(kind, slot, blocks - 2, UNIT).wait()
        out_copy(kind, slot, blocks - 1, last).wait()

    pair = pltpu.make_async_remote_copy(
        src_ref=spread.at[1 - core],
        dst_ref=pair_in,
        send_sem=pair_sem.at[0],
        recv_sem=pair_sem.at[1],
        device_id=(other_core, col),
        device_id_type=MESH,
    )

    def chip_copy(step):
        return pltpu.make_async_remote_copy(
            src_ref=spread.at[core, lax.rem(chip + step, chips)],
            dst_ref=chip_in.at[step - 1],
            send_sem=chip_sem.at[0, step - 1],
            recv_sem=chip_sem.at[1, step - 1],
            device_id=(chip_peer(step), col),
            device_id_type=MESH,
        )

    def phase_back(j, carry):
        arrive(3, 0, j)
        arrive(3, 1, j)

        def term(n, c):
            i, a = lax.rem(n, 2), lax.div(n, 2)
            acc[half_rows(a), :] += lax.dot_general(
                results[i, j, a].reshape(2 * quarter, UNIT),
                weights[i, block_rows(j), :],
                plain,
                preferred_element_type=jnp.float32,
            )
            return c

        lax.fori_loop(0, 4, term, 0)

        @pl.when(j == blocks - 1)
        def _():
            weights[2, pl.ds(0, tokens), :] = acc[...].astype(jnp.bfloat16)

            def place(owner, c):
                wanted = held_ref[pl.ds(owner, 1), :]
                ids = lax.broadcasted_iota(jnp.int32, (tokens, slots), 0)
                spread[lax.rem(owner, 2), lax.div(owner, 2)] = lax.dot_general(
                    (ids == wanted).astype(jnp.bfloat16),
                    weights[2, pl.ds(0, tokens), :],
                    down,
                    preferred_element_type=jnp.float32,
                ).astype(jnp.bfloat16)
                return c

            lax.fori_loop(0, row_count, place, 0)
            pair.start()

        def both(i, c):
            emit(i, j, (0, 1), i, 0)
            return c

        return lax.fori_loop(0, 2, both, carry)

    lax.fori_loop(0, blocks, phase_back, 0)
    pair.wait_recv()
    spread[core] = (
        spread[core].astype(jnp.float32) + pair_in[...].astype(jnp.float32)
    ).astype(jnp.bfloat16)
    for step in range(1, chips):
        chip_copy(step).start()

    def phase_relay(j, carry):
        arrive(2, 2, j)
        start(3, 2, j)
        return carry

    lax.fori_loop(0, blocks, phase_relay, 0)
    drain(0, 0)
    drain(1, 1)

    def phase_last(j, carry):
        arrive(3, 2, j)
        emit(2, j, (2,), 0, 1)
        return carry

    lax.fori_loop(0, blocks, phase_last, 0)
    total = spread[core, chip].astype(jnp.float32)
    for step in range(1, chips):
        chip_copy(step).wait_recv()
        total = total + chip_in[step - 1].astype(jnp.float32)
    gi_ref[...] = total.astype(jnp.bfloat16)

    def phase_sent(j, carry):
        for step in range(4):
            for i in range(3):
                each_way(i, j, lambda way: copy(step, i, j, way).wait_send())
        return carry

    lax.fori_loop(0, blocks, phase_sent, 0)
    pair.wait_send()
    for step in range(1, chips):
        chip_copy(step).wait_send()
    drain(2, 0)


def fused_layer(
    tokens, call_id, packed, cot_cols, weights, target, held_at, gate_weight, up_weight, down_weight
):
    units, width = down_weight.shape
    row_count = lax.axis_size("row")
    chips = row_count // 2
    slots = held_at.shape[0] // row_count
    blocks = -(-units // UNIT)
    quarter = tokens // 4
    low = jnp.bfloat16
    any_space = pl.BlockSpec(memory_space=pl.ANY)
    vmem = pl.BlockSpec(memory_space=pltpu.VMEM)
    whole = jax.ShapeDtypeStruct((units, width), low)
    grad_input, grad_gate, grad_up, grad_down = pl.pallas_call(
        functools.partial(fused_kernel, (tokens, units, blocks)),
        out_shape=[jax.ShapeDtypeStruct((slots, width), low), whole, whole, whole],
        in_specs=[
            any_space,
            any_space,
            pl.BlockSpec(memory_space=pltpu.SMEM),
            vmem,
            vmem,
            any_space,
            any_space,
            any_space,
        ],
        out_specs=[vmem, any_space, any_space, any_space],
        scratch_shapes=[
            pltpu.VMEM((3, max(blocks * UNIT, tokens), width), low),
            pltpu.VMEM((2, tokens, width), low),
            pltpu.VMEM((max(row_count * cot_cols.shape[0], 4 * UNIT), width), low),
            pltpu.VMEM((3, blocks, 2, 2, quarter, UNIT), low),
            pltpu.VMEM((3, blocks, 2, quarter, UNIT), low),
            pltpu.VMEM((3, blocks, quarter, UNIT), low),
            pltpu.VMEM((3, blocks, 2, 2, quarter, UNIT), low),
            pltpu.VMEM((tokens, width), jnp.float32),
            pltpu.VMEM((2, chips, slots, width), low),
            pltpu.VMEM((chips, slots, width), low),
            pltpu.VMEM((chips - 1, slots, width), low),
            pltpu.SemaphoreType.DMA((4, 3, blocks)),
            pltpu.SemaphoreType.DMA((4, 3, blocks)),
            pltpu.SemaphoreType.DMA((3, blocks)),
            pltpu.SemaphoreType.DMA((2,)),
            pltpu.SemaphoreType.DMA((3, row_count)),
            pltpu.SemaphoreType.DMA((row_count,)),
            pltpu.SemaphoreType.DMA((2, 2)),
            pltpu.SemaphoreType.DMA((2,)),
            pltpu.SemaphoreType.DMA((2, chips - 1)),
        ],
        compiler_params=pltpu.CompilerParams(
            collective_id=call_id, has_side_effects=True, vmem_limit_bytes=67_000_000
        ),
        cost_estimate=pl.CostEstimate(
            flops=16 * tokens * width * units, bytes_accessed=12 * width * units, transcendentals=0
        ),
    )(
        packed,
        cot_cols,
        weights,
        target,
        held_at.reshape(row_count, slots),
        gate_weight.T,
        up_weight.T,
        down_weight,
    )
    return grad_input, grad_gate.T, grad_up.T, grad_down


def column_sum(a, bs):
    dims = (((1,), (1,)), ((), ()))
    return [
        lax.psum(
            lax.dot_general(a, b, dims, preferred_element_type=jnp.float32).astype(jnp.bfloat16),
            "col",
        )
        for b in bs
    ]


def per_device(
    roll_hidden,
    roll_cotangent,
    lengths,
    owners,
    prompts,
    rewards,
    gate_weight,
    up_weight,
    down_weight,
):
    row_count = lax.axis_size("row")
    col_count = lax.axis_size("col")
    total_tokens = row_count * CAPR
    count_prompts = row_count * col_count // 8
    slot_count = roll_hidden.shape[0]
    width = roll_hidden.shape[1] // col_count
    local = jnp.stack(
        [
            lengths.astype(jnp.float32),
            owners.astype(jnp.float32),
            prompts.astype(jnp.float32),
            rewards,
        ],
        axis=1,
    )
    fused = col_count == 4 and row_count % 2 == 0 and row_count >= 4
    if fused:
        table, packed, cot_cols, spots = gather_rows(
            local, roll_hidden, roll_cotangent, total_tokens
        )
        table = table[:, 0, :]
    else:
        table = gather_table(local)
    all_lengths = table[:, 0].astype(jnp.int32)
    all_owners = table[:, 1].astype(jnp.int32)
    all_prompts = table[:, 2].astype(jnp.int32)
    weights = row_weights(all_lengths, all_prompts, table[:, 3], count_prompts)
    offsets = row_offsets(all_lengths, all_owners)
    starts = jnp.cumsum(all_lengths) - all_lengths
    live_total = jnp.sum(all_lengths)
    firsts = all_owners * CAPR + offsets
    places = jnp.arange(total_tokens, dtype=jnp.int32)[:, None]
    inside = (places >= firsts[None, :]) & (places < (firsts + all_lengths)[None, :])
    held_at = jnp.sum(jnp.where(inside, places + (starts - firsts + 1)[None, :], 0), 1) - 1

    if fused:
        sizes = [total_tokens * part // 16 for part in SIZES] + [total_tokens]
        return lax.switch(
            sum((live_total > size).astype(jnp.int32) for size in sizes[:-1]),
            [functools.partial(fused_layer, size, 3 + i) for i, size in enumerate(sizes)],
            packed,
            cot_cols,
            weights,
            spots,
            held_at,
            gate_weight,
            up_weight,
            down_weight,
        )
    slots = jnp.arange(slot_count, dtype=jnp.int32)
    target = jnp.where(
        slots[None, :] < all_lengths[:, None], starts[:, None] + slots[None, :], total_tokens
    ).reshape(-1)
    slot_weights = jnp.repeat(weights, slot_count)
    def to_cols(rolled):
        blocks = rolled.reshape(slot_count, col_count, width)
        return lax.all_to_all(blocks, "col", split_axis=1, concat_axis=0, tiled=True).reshape(
            col_count * slot_count, width
        )

    hidden_cols, roll_cotangent = lax.optimization_barrier((to_cols(roll_hidden), roll_cotangent))
    hidden_all = lax.all_gather(hidden_cols, "row", axis=0, tiled=True)
    operands = (
        hidden_all,
        to_cols(roll_cotangent),
        target,
        slot_weights,
        held_at,
        gate_weight,
        up_weight,
        down_weight,
    )
    return layer(total_tokens, *operands)


def layer(
    tokens,
    hidden_all,
    cotangent_cols,
    target,
    slot_weights,
    held_at,
    gate_weight,
    up_weight,
    down_weight,
):
    ids = jnp.arange(tokens, dtype=jnp.int32)
    pick = (ids[:, None] == target[None, :]).astype(jnp.bfloat16)
    spread_out = (held_at[:, None] == ids[None, :]).astype(jnp.bfloat16)

    def move(onehot, every):
        return jnp.dot(onehot, every, preferred_element_type=jnp.float32).astype(jnp.bfloat16)

    cotangent_all = lax.all_gather(cotangent_cols, "row", axis=0, tiled=True)
    packed = move(pick, hidden_all)
    gate, upval = column_sum(packed, (gate_weight.T, up_weight.T))
    slot_weights, gate, upval = lax.optimization_barrier((slot_weights, gate, upval))
    packed_grad = move(
        pick, (cotangent_all.astype(jnp.float32) * slot_weights[:, None]).astype(jnp.bfloat16)
    )
    (grad_hidden,) = column_sum(packed_grad, (down_weight,))
    gate, upval, grad_hidden = (v.astype(jnp.float32) for v in (gate, upval, grad_hidden))
    sig = jax.nn.sigmoid(gate)
    silu = gate * sig
    hidden = (silu * upval).astype(jnp.bfloat16)
    contract_cols = (((1,), (1,)), ((), ()))
    grad_gate_act = (grad_hidden * upval * sig * (1.0 + gate * (1.0 - sig))).astype(jnp.bfloat16)
    grad_up_act = (grad_hidden * silu).astype(jnp.bfloat16)
    contract_rows = (((0,), (0,)), ((), ()))
    grad_down = lax.dot_general(
        hidden, packed_grad, contract_rows, preferred_element_type=jnp.float32
    ).astype(jnp.bfloat16)
    grad_gate = lax.dot_general(
        packed, grad_gate_act, contract_rows, preferred_element_type=jnp.float32
    ).astype(jnp.bfloat16)
    grad_up = lax.dot_general(
        packed, grad_up_act, contract_rows, preferred_element_type=jnp.float32
    ).astype(jnp.bfloat16)
    term = lax.dot_general(
        grad_gate_act, gate_weight, contract_cols, preferred_element_type=jnp.float32
    )
    term = (
        term
        + lax.dot_general(
            grad_up_act, up_weight, contract_cols, preferred_element_type=jnp.float32
        )
    ).astype(jnp.bfloat16)
    grad_input = lax.psum_scatter(
        move(spread_out, term), "row", scatter_dimension=0, tiled=True
    )
    return (grad_input, grad_gate, grad_up, grad_down)


def solution(mesh):
    return jax.shard_map(
        per_device,
        mesh=mesh,
        in_specs=(
            P(("row", "col"), None),
            P(("row", "col"), None),
            P(("row", "col")),
            P(("row", "col")),
            P(("row", "col")),
            P(("row", "col")),
            P("col", "row"),
            P("col", "row"),
            P("row", "col"),
        ),
        out_specs=(P("row", "col"), P("col", "row"), P("col", "row"), P("row", "col")),
        check_vma=False,
    )
```

```python
import functools

import jax
import jax.numpy as jnp
from jax import lax
from jax.experimental import pallas as pl
from jax.experimental.pallas import tpu as pltpu
from jax.sharding import PartitionSpec as P

CAPR = 128
MESH = pl.DeviceIdType.MESH
SIZES = (12, 13, 14)


spread_floor = 0.7


def row_weights(lengths, prompts, rewards, count_prompts):
    onehot = (prompts[:, None] == jnp.arange(count_prompts, dtype=jnp.int32)[None, :]).astype(
        jnp.float32
    )
    counts = jnp.maximum(jnp.sum(onehot, 0), 1.0)
    means = jnp.sum(onehot * rewards[:, None], 0) / counts
    centred = rewards - jnp.sum(onehot * means[None, :], 1)
    spreads = jnp.sqrt(jnp.sum(onehot * (centred * centred)[:, None], 0) / counts)
    divisor = jnp.maximum(jnp.sum(onehot * spreads[None, :], 1), spread_floor)
    return centred / divisor / lengths.astype(jnp.float32)


def row_offsets(lengths, owners):
    count = lengths.shape[0]
    places = jnp.arange(count, dtype=jnp.int32)
    earlier = (owners[None, :] == owners[:, None]) & (places[None, :] < places[:, None])
    return jnp.sum(jnp.where(earlier, lengths[None, :], 0), 1)


def table_kernel(mine_ref, all_ref, send_sem, recv_sem, own_sem):
    row, col = lax.axis_index("row"), lax.axis_index("col")
    row_count, col_count = lax.axis_size("row"), lax.axis_size("col")
    barrier = pltpu.get_barrier_semaphore()

    def col_peer(step):
        return (row, lax.rem(col + step, col_count))

    def row_peer(step):
        return (lax.rem(row + step, row_count), col)

    for step in range(1, col_count):
        pl.semaphore_signal(barrier, inc=1, device_id=col_peer(step), device_id_type=MESH)
    for step in range(1, row_count):
        pl.semaphore_signal(barrier, inc=1, device_id=row_peer(step), device_id_type=MESH)
    own = pltpu.make_async_copy(mine_ref, all_ref.at[row * col_count + col], own_sem)
    own.start()
    pl.semaphore_wait(barrier, col_count + row_count - 2)
    copies = [
        pltpu.make_async_remote_copy(
            src_ref=mine_ref,
            dst_ref=all_ref.at[row * col_count + col],
            send_sem=send_sem.at[step],
            recv_sem=recv_sem.at[step],
            device_id=col_peer(step),
            device_id_type=MESH,
        )
        for step in range(1, col_count)
    ]
    for copy in copies:
        copy.start()
    own.wait()
    for copy in copies:
        copy.wait_recv()
    held = all_ref.at[pl.ds(row * col_count, col_count)]
    onward = [
        pltpu.make_async_remote_copy(
            src_ref=held,
            dst_ref=held,
            send_sem=send_sem.at[col_count + step],
            recv_sem=recv_sem.at[col_count + step],
            device_id=row_peer(step),
            device_id_type=MESH,
        )
        for step in range(1, row_count)
    ]
    for copy in onward:
        copy.start()
    for copy in onward:
        copy.wait_recv()
    for copy in copies + onward:
        copy.wait_send()


def gather_table(local):
    row_count, col_count = lax.axis_size("row"), lax.axis_size("col")
    devices = row_count * col_count
    mine = jnp.pad(local, ((0, 0), (0, 128 - local.shape[1])))
    every = pl.pallas_call(
        table_kernel,
        out_shape=jax.ShapeDtypeStruct((devices, 1, 128), jnp.float32),
        in_specs=[pl.BlockSpec(memory_space=pltpu.VMEM)],
        out_specs=pl.BlockSpec(memory_space=pltpu.VMEM),
        scratch_shapes=[
            pltpu.SemaphoreType.DMA((row_count + col_count,)),
            pltpu.SemaphoreType.DMA((row_count + col_count,)),
            pltpu.SemaphoreType.DMA,
        ],
        compiler_params=pltpu.CompilerParams(collective_id=2, has_side_effects=True),
    )(mine)
    return every[:, 0, : local.shape[1]]


UNIT = 384


def padded_slots(slots):
    return -(-slots // 16) * 16


class Line:
    def __init__(self, every, size, send_sem, recv_sem, pieces):
        self.every, self.send_sem, self.recv_sem, self.pieces = every, send_sem, recv_sem, pieces
        self.size = size
        row, self.col = lax.axis_index("row"), lax.axis_index("col")
        self.chips = lax.axis_size("row") // 2
        self.core, self.chip = lax.rem(row, 2), lax.div(row, 2)

    def place(self, r, c):
        first = pl.multiple_of((r * self.pieces + c) * self.size, self.size)
        return self.every.at[pl.ds(first, self.size)]

    def hop(self, way, r, c):
        index = (r, c) if self.pieces > 1 else (r,)
        target = (
            (self.chip + 1) * 2 + self.core,
            (self.chip - 1) * 2 + self.core,
            self.chip * 2 + 1 - self.core,
        )[way]
        place = self.place(r, c)
        return pltpu.make_async_remote_copy(
            src_ref=place,
            dst_ref=place,
            send_sem=self.send_sem.at[(way,) + index],
            recv_sem=self.recv_sem.at[index],
            device_id=(target, self.col),
            device_id_type=MESH,
        )

    def has(self, way):
        return (self.chip + 1 < self.chips, self.chip > 0)[way]

    def offer(self, r, c):
        for way in range(2):
            pl.when(self.has(way))(lambda: self.hop(way, r, c).start())
        self.hop(2, r, c).start()

    def there(self, d, side):
        source = self.chip + d if side else self.chip - d
        return source, (source < self.chips) if side else (source >= 0)

    def arrival(self, step):
        if self.pieces == 1:
            return 0
        return lax.rem(self.col + self.pieces - step, self.pieces)

    def pass_on(self, d):
        for c in map(self.arrival, range(self.pieces)):
            for side in range(2):
                source, valid = self.there(d, side)
                r = source * 2 + self.core

                @pl.when(valid)
                def _():
                    self.hop(2, r, c).wait_recv()
                    pl.when(self.has(side))(lambda: self.hop(side, r, c).start())
                    self.hop(2, r, c).start()

    def partner(self, source):
        for c in range(self.pieces):
            self.hop(2, source * 2 + 1 - self.core, c).wait_recv()

    def sent(self):
        def chip_sent(source, carry):
            r = source * 2 + self.core
            for c in range(self.pieces):

                @pl.when((source <= self.chip) & (self.chip + 1 < self.chips))
                def _():
                    self.hop(0, r, c).wait_send()

                @pl.when((source >= self.chip) & (self.chip > 0))
                def _():
                    self.hop(1, r, c).wait_send()

                self.hop(2, r, c).wait_send()
            return carry

        lax.fori_loop(0, self.chips, chip_sent, 0)


def gather_kernel(
    sizes,
    mine_ref,
    hidden_ref,
    cotangent_ref,
    choice_ref,
    packed_ref,
    cot_ref,
    target_ref,
    held_ref,
    weight_ref,
    table_ref,
    raw,
    hidden_mine,
    cot_mine,
    every,
    table_sems,
    own_sem,
    raw_sem,
    cols_sems,
    line_send,
    line_recv,
):
    row, col = lax.axis_index("row"), lax.axis_index("col")
    row_count, col_count = lax.axis_size("row"), lax.axis_size("col")
    slots = hidden_ref.shape[0]
    pad, width = hidden_mine.shape[1:]
    raw_copies = [
        pltpu.make_async_copy(source, raw.at[i], raw_sem.at[i])
        for i, source in enumerate((hidden_ref, cotangent_ref))
    ]
    for move in raw_copies:
        move.start()
    line = Line(every, pad, line_send, line_recv, col_count)

    def col_peer(step):
        return (row, lax.rem(col + step, col_count))

    def row_peer(step):
        return (lax.rem(row + step, row_count), col)

    barrier = pltpu.get_barrier_semaphore()
    for step in range(1, col_count):
        pl.semaphore_signal(barrier, inc=1, device_id=col_peer(step), device_id_type=MESH)
    for step in range(1, row_count):
        pl.semaphore_signal(barrier, inc=1, device_id=row_peer(step), device_id_type=MESH)
    own = pltpu.make_async_copy(mine_ref, table_ref.at[row * col_count + col], own_sem)
    own.start()
    for i, held in enumerate((hidden_mine, cot_mine)):
        raw_copies[i].wait()
        for c in range(col_count):
            if pad > slots:
                held[c, pl.ds(pad - 16, 16), :] = jnp.zeros((16, width), held.dtype)
            held[c, pl.ds(0, slots), :] = raw[i, :, pl.ds(c * width, width)]
    mine_at = pl.multiple_of((row * col_count + col) * pad, pad)
    cot_at = pl.multiple_of(col * pad, pad)
    every[pl.ds(mine_at, pad), :] = hidden_mine[col]
    cot_ref[pl.ds(cot_at, pad), :] = cot_mine[col]
    pl.semaphore_wait(barrier, col_count + row_count - 2)

    def table_copy(kind, step, place, target):
        return pltpu.make_async_remote_copy(
            src_ref=place,
            dst_ref=place,
            send_sem=table_sems.at[0, kind, step],
            recv_sem=table_sems.at[1, kind, step],
            device_id=target,
            device_id_type=MESH,
        )

    def cols_copy(kind, step):
        held = (hidden_mine, cot_mine)[kind]
        place = every.at[pl.ds(mine_at, pad)] if kind == 0 else cot_ref.at[pl.ds(cot_at, pad)]
        return pltpu.make_async_remote_copy(
            src_ref=held.at[lax.rem(col + step, col_count)],
            dst_ref=place,
            send_sem=cols_sems.at[kind, 0, step],
            recv_sem=line_recv.at[row, col] if kind == 0 else cols_sems.at[kind, 1, step],
            device_id=col_peer(step),
            device_id_type=MESH,
        )

    own.wait()
    table_cols = [
        table_copy(0, step, table_ref.at[row * col_count + col], col_peer(step))
        for step in range(1, col_count)
    ]
    for move in table_cols:
        move.start()
    hidden_cols = [cols_copy(0, step) for step in range(1, col_count)]
    cot_cols = [cols_copy(1, step) for step in range(1, col_count)]
    for move in hidden_cols:
        move.start()
    line.offer(row, col)
    for move in cot_cols:
        move.start()
    for move in table_cols:
        move.wait_recv()
    held_rows = table_ref.at[pl.ds(row * col_count, col_count)]
    table_rows = [
        table_copy(1, step, held_rows, row_peer(step)) for step in range(1, row_count)
    ]
    for move in table_rows:
        move.start()
    for c in map(line.arrival, range(1, col_count)):
        line.hop(2, row, c).wait_recv()
        line.offer(row, c)
    line.pass_on(1)
    for move in table_rows:
        move.wait_recv()

    count = row_count * col_count
    tokens = packed_ref.shape[0]
    table = table_ref[...].reshape(count, 128)
    lengths, owners, prompts, rewards = (table[:, i : i + 1] for i in range(4))
    across = lax.broadcasted_iota(jnp.int32, (count, count), 1)
    below = lax.broadcasted_iota(jnp.int32, (count, count), 0)

    def as_row(column):
        return jnp.sum(jnp.where(across == below, column, 0.0), 0, keepdims=True)

    lengths_row = as_row(lengths)
    starts = jnp.sum(jnp.where(across < below, lengths_row, 0.0), 1, keepdims=True)
    lanes = lax.broadcasted_iota(jnp.int32, (count, count * pad), 1)
    rows = lax.broadcasted_iota(jnp.int32, (count, count * pad), 0)
    spot = (lanes - rows * pad).astype(jnp.float32)
    live = (spot >= 0.0) & (spot < lengths)
    spots = jnp.sum(jnp.where(live, starts + spot + 1.0, 0.0), 0, keepdims=True) - 1.0
    target_ref[...] = spots.astype(jnp.int32)

    earlier = (as_row(owners) == owners) & (across < below)
    offsets = jnp.sum(jnp.where(earlier, lengths_row, 0.0), 1, keepdims=True)
    firsts = owners * float(CAPR) + offsets
    places = lax.broadcasted_iota(jnp.int32, (count, tokens), 1).astype(jnp.float32)
    inside = (places >= firsts) & (places < firsts + lengths)
    held = jnp.sum(jnp.where(inside, places + (starts - firsts + 1.0), 0.0), 0, keepdims=True)
    held_ref[...] = (held - 1.0).astype(jnp.int32)

    kinds = lax.broadcasted_iota(jnp.int32, (count, 128), 1).astype(jnp.float32)
    onehot = (prompts == kinds).astype(jnp.float32)
    counts = jnp.maximum(jnp.sum(onehot, 0, keepdims=True), 1.0)
    means = jnp.sum(onehot * rewards, 0, keepdims=True) / counts
    centred = rewards - jnp.sum(onehot * means, 1, keepdims=True)
    spreads = jnp.sqrt(jnp.sum(onehot * (centred * centred), 0, keepdims=True) / counts)
    divisor = jnp.maximum(jnp.sum(onehot * spreads, 1, keepdims=True), spread_floor)
    weight_ref[...] = as_row(centred / divisor / lengths)
    total = jnp.sum(lengths, 0, keepdims=True)
    choice = sum((total > float(size)).astype(jnp.int32) for size in sizes)
    choice_ref[...] = jnp.broadcast_to(choice, choice_ref.shape)

    packed_ref[...] = jnp.zeros_like(packed_ref)
    chip_rows = 2 * col_count * pad
    half = tokens // 4

    def gathered(d, carry):
        @pl.when((d > 0) & (d + 1 < line.chips))
        def _():
            line.pass_on(d + 1)

        def take(side, c):
            source = line.chip + jnp.where(side == 1, d, -d)
            valid = (source >= 0) & (source < line.chips) & ((d > 0) | (side == 0))

            @pl.when(valid)
            def _():
                line.partner(source)
                where = pl.ds(pl.multiple_of(source * chip_rows, 128), chip_rows)
                wanted = target_ref[:, where]
                block = every[where, :]

                def part(n, c):
                    place = pl.ds(pl.multiple_of(n * half, half), half)
                    ids = lax.broadcasted_iota(jnp.int32, (half, chip_rows), 0) + n * half
                    pick = (ids == wanted).astype(jnp.bfloat16)
                    moved = jnp.dot(pick, block, preferred_element_type=jnp.float32)
                    held_now = packed_ref[place, :].astype(jnp.float32)
                    packed_ref[place, :] = (held_now + moved).astype(packed_ref.dtype)
                    return c

                lax.fori_loop(0, 4, part, 0)

            return c

        return lax.fori_loop(0, 2, take, carry)

    lax.fori_loop(0, line.chips, gathered, 0)
    for move in cot_cols:
        move.wait_recv()
    for move in table_cols + table_rows + hidden_cols + cot_cols:
        move.wait_send()
    line.sent()


def gather_rows(local, roll_hidden, roll_cotangent, total_tokens, sizes):
    row_count, col_count = lax.axis_size("row"), lax.axis_size("col")
    devices = row_count * col_count
    slots, whole = roll_hidden.shape
    width = whole // col_count
    pad = padded_slots(slots)
    low = roll_hidden.dtype
    mine = jnp.pad(local, ((0, 0), (0, 128 - local.shape[1])))
    vmem = pl.BlockSpec(memory_space=pltpu.VMEM)
    any_space = pl.BlockSpec(memory_space=pltpu.HBM)
    steps = max(row_count, col_count)
    return pl.pallas_call(
        functools.partial(gather_kernel, sizes),
        out_shape=[
            jax.ShapeDtypeStruct((1, 128), jnp.int32),
            jax.ShapeDtypeStruct((total_tokens, width), low),
            jax.ShapeDtypeStruct((col_count * pad, width), low),
            jax.ShapeDtypeStruct((1, devices * pad), jnp.int32),
            jax.ShapeDtypeStruct((1, total_tokens), jnp.int32),
            jax.ShapeDtypeStruct((1, devices), jnp.float32),
        ],
        in_specs=[vmem, any_space, any_space],
        out_specs=[vmem] * 6,
        scratch_shapes=[
            pltpu.VMEM((devices, 1, 128), jnp.float32),
            pltpu.VMEM((2, slots, whole), low),
            pltpu.VMEM((col_count, pad, width), low),
            pltpu.VMEM((col_count, pad, width), low),
            pltpu.VMEM((row_count * col_count * pad, width), low),
            pltpu.SemaphoreType.DMA((2, 2, steps)),
            pltpu.SemaphoreType.DMA,
            pltpu.SemaphoreType.DMA((2,)),
            pltpu.SemaphoreType.DMA((2, 2, col_count)),
            pltpu.SemaphoreType.DMA((3, row_count, col_count)),
            pltpu.SemaphoreType.DMA((row_count, col_count)),
        ],
        compiler_params=pltpu.CompilerParams(
            collective_id=2, has_side_effects=True, vmem_limit_bytes=67_000_000
        ),
    )(mine, roll_hidden, roll_cotangent)


def fused_kernel(
    dims,
    pk_ref,
    cot_ref,
    weight_ref,
    target_ref,
    held_ref,
    gw_ref,
    uw_ref,
    dw_ref,
    gi_ref,
    gg_ref,
    gu_ref,
    hid_ref,
    pg_ref,
    weights,
    tokens_held,
    every,
    parts,
    first_in,
    second_in,
    results,
    acc,
    spread,
    pair_in,
    chip_in,
    send_sem,
    recv_sem,
    weight_sem,
    held_sem,
    line_send,
    line_recv,
    out_sem,
    pair_sem,
    chip_sem,
):
    tokens, units, blocks = dims
    quarter = tokens // 4
    row, col = lax.axis_index("row"), lax.axis_index("col")
    row_count, col_count = lax.axis_size("row"), lax.axis_size("col")
    chips = row_count // 2
    x, y = lax.rem(col, 2), lax.div(col, 2)
    core, chip = lax.rem(row, 2), lax.div(row, 2)
    x_peer, y_peer = y * 2 + (1 - x), (1 - y) * 2 + x
    other_core = chip * 2 + 1 - core
    last = units - (blocks - 1) * UNIT
    slots = held_ref.shape[1] // row_count
    width = cot_ref.shape[1]
    pad = cot_ref.shape[0] // col_count
    line = Line(every, col_count * pad, line_send, line_recv, 1)

    def load(i, j, size):
        place = pl.ds(j * UNIT, size)
        return pltpu.make_async_copy(
            (gw_ref, uw_ref, dw_ref)[i].at[place], weights.at[i, place], weight_sem.at[i, j]
        )

    def block_size(j):
        return UNIT if j < blocks - 1 else last

    bring = pltpu.make_async_copy(
        pk_ref.at[pl.ds(0, tokens)], tokens_held.at[0], held_sem.at[0]
    )
    bring_cot = pltpu.make_async_copy(cot_ref, line.place(row, 0), held_sem.at[1])
    bring.start()
    for j in range(blocks):
        for i in range(2):
            load(i, j, block_size(j)).start()
        if j == 0:
            bring_cot.start()
    for j in range(blocks):
        load(2, j, block_size(j)).start()

    def chip_peer(step):
        return lax.rem(chip + step, chips) * 2 + core

    barrier = pltpu.get_barrier_semaphore()
    for peer in (x_peer, y_peer):
        pl.semaphore_signal(barrier, inc=1, device_id=(row, peer), device_id_type=MESH)
    pl.semaphore_signal(barrier, inc=1, device_id=(other_core, col), device_id_type=MESH)
    for step in range(1, chips):
        pl.semaphore_signal(
            barrier, inc=1, device_id=(chip_peer(step), col), device_id_type=MESH
        )
    if blocks * UNIT > units:
        for i in range(3):
            weights[i, pl.ds(units, blocks * UNIT - units), :] = jnp.zeros(
                (blocks * UNIT - units, width), weights.dtype
            )
    pl.semaphore_wait(barrier, 2 + chips)

    def copy(step, i, j, way):
        if step == 0:
            src = parts.at[i, j, 1 - x] if way == 0 else parts.at[i, j, :, 1 - y]
            dst = first_in.at[i, j]
        elif step == 1:
            src = parts.at[i, j, x, 1 - y] if way == 0 else parts.at[i, j, 1 - x, y]
            dst = second_in.at[i, j]
        elif step == 2:
            src = dst = results.at[i, j, x, y]
        else:
            src = dst = results.at[i, j, x] if way == 0 else results.at[i, j, :, y]
        along_x = (way == 0) == (step in (0, 3))
        return pltpu.make_async_remote_copy(
            src_ref=src,
            dst_ref=dst,
            send_sem=send_sem.at[step, i, j],
            recv_sem=recv_sem.at[step, i, j],
            device_id=(row, x_peer if along_x else y_peer),
            device_id_type=MESH,
        )

    def each_way(i, j, act):
        if isinstance(i, int) and i < 2:
            act(i)
        else:
            chosen = i if not isinstance(i, int) else lax.rem(j, 2)
            for way in range(2):
                pl.when(chosen == way)(functools.partial(act, way))

    def start(step, i, j):
        each_way(i, j, lambda way: copy(step, i, j, way).start())

    def arrive(step, i, j):
        each_way(i, j, lambda way: copy(step, i, j, way).wait_recv())

    def block_rows(j):
        return pl.ds(pl.multiple_of(j * UNIT, 128), UNIT)

    def half_rows(a):
        return pl.ds(pl.multiple_of(a * 2 * quarter, 2 * quarter), 2 * quarter)

    across = (((1,), (1,)), ((), ()))
    plain = (((1,), (0,)), ((), ()))
    down = (((0,), (0,)), ((), ()))

    def loaded(i, j):
        for which in range(3):

            @pl.when((i == which) & (j < blocks - 1))
            def _():
                load(which, j, UNIT).wait()

            @pl.when((i == which) & (j == blocks - 1))
            def _():
                load(which, j, last).wait()

    def forward(i, j, which):
        loaded(i, j)

        def part(a, c):
            term = lax.dot_general(
                tokens_held[which, half_rows(a), :],
                weights[i, block_rows(j), :],
                across,
                preferred_element_type=jnp.float32,
            )
            parts[i, j, a] = term.astype(jnp.bfloat16).reshape(2, quarter, UNIT)
            return c

        lax.fori_loop(0, 2, part, 0)
        start(0, i, j)

    def halve(i, j):
        def act(way):
            copy(0, i, j, way).wait_recv()
            if way == 0:
                total = parts[i, j, x, 1 - y].astype(jnp.float32)
                total = total + first_in[i, j, 1 - y].astype(jnp.float32)
                parts[i, j, x, 1 - y] = total.astype(jnp.bfloat16)
            else:
                total = parts[i, j, 1 - x, y].astype(jnp.float32)
                total = total + first_in[i, j, 1 - x].astype(jnp.float32)
                parts[i, j, 1 - x, y] = total.astype(jnp.bfloat16)
            copy(1, i, j, way).start()

        each_way(i, j, act)

    def own_sum(i, j):
        arrive(1, i, j)
        place = (y, x)[i] if i < 2 else lax.rem(j, 2) * x + (1 - lax.rem(j, 2)) * y
        return (
            parts[i, j, x, y].astype(jnp.float32)
            + first_in[i, j, place].astype(jnp.float32)
            + second_in[i, j].astype(jnp.float32)
        )

    bring.wait()
    bring_cot.wait()

    def phase_up(n, carry):
        forward(lax.rem(n, 2), lax.div(n, 2), 0)

        @pl.when(n == 0)
        def _():
            line.offer(row, 0)

        return carry

    lax.fori_loop(0, 2 * blocks, phase_up, 0)
    acc[...] = jnp.zeros_like(acc)

    def phase_up_halve(j, carry):
        @pl.when((j >= 1) & (j < chips))
        def _():
            line.pass_on(j)

        halve(0, j)
        halve(1, j)
        return carry

    def some_halves(first, end):
        lax.fori_loop(first, end, phase_up_halve, 0)

    early = min(chips, blocks)
    some_halves(0, early)
    for d in range(early, chips):
        line.pass_on(d)

    def partners(source, carry):
        line.partner(source)
        return carry

    lax.fori_loop(0, chips, partners, 0)
    line.sent()

    def scale(k, carry):
        where = pl.ds(pl.multiple_of(k * pad, pad), pad)
        scaled = every[where, :].astype(jnp.float32) * weight_ref[0, k]
        every[where, :] = scaled.astype(jnp.bfloat16)
        return carry

    lax.fori_loop(0, row_count * col_count, scale, 0)

    def pick(n, carry):
        place = pl.ds(pl.multiple_of(n * quarter, quarter), quarter)
        ids = lax.broadcasted_iota(jnp.int32, (quarter, target_ref.shape[1]), 0) + n * quarter
        tokens_held[1, place, :] = jnp.dot(
            (ids == target_ref[...]).astype(jnp.bfloat16),
            every[pl.ds(0, target_ref.shape[1]), :],
            preferred_element_type=jnp.float32,
        ).astype(jnp.bfloat16)
        return carry

    lax.fori_loop(0, 4, pick, 0)
    keep_grad = pltpu.make_async_copy(tokens_held.at[1], pg_ref, held_sem.at[0])
    keep_grad.start()

    def phase_down(j, carry):
        forward(2, j, 1)
        return carry

    lax.fori_loop(0, blocks, phase_down, 0)
    some_halves(early, blocks)

    def phase_down_halve(j, carry):
        halve(2, j)
        return carry

    lax.fori_loop(0, blocks, phase_down_halve, 0)

    def phase_own(j, carry):
        gate, upval, grad_hidden = (own_sum(i, j) for i in range(3))
        sig = jax.nn.sigmoid(gate)
        silu = gate * sig
        results[2, j, x, y] = (silu * upval).astype(jnp.bfloat16)
        results[0, j, x, y] = (grad_hidden * upval * sig * (1.0 + gate * (1.0 - sig))).astype(
            jnp.bfloat16
        )
        results[1, j, x, y] = (grad_hidden * silu).astype(jnp.bfloat16)
        start(2, 0, j)
        start(2, 1, j)

        @pl.when(j > 0)
        def _():
            for i in range(2):
                arrive(2, i, j - 1)
                start(3, i, j - 1)

        return carry

    lax.fori_loop(0, blocks, phase_own, 0)
    for i in range(2):
        arrive(2, i, blocks - 1)
        start(3, i, blocks - 1)

    def phase_share(j, carry):
        start(2, 2, j)
        return carry

    lax.fori_loop(0, blocks, phase_share, 0)

    def staged(slot, j, size):
        return pl.ds(pl.multiple_of((slot * 2 + lax.rem(j, 2)) * UNIT, UNIT), size)

    def out_copy(which, i, j, size):
        return pltpu.make_async_copy(
            every.at[staged(i, j, size)],
            (gg_ref, gu_ref)[which].at[pl.ds(pl.multiple_of(j * UNIT, 128), size)],
            out_sem.at[i, lax.rem(j, 2)],
        )

    def emit(i, j):
        @pl.when(j > 1)
        def _():
            out_copy(0, i, j - 2, UNIT).wait()

        every[staged(i, j, UNIT), :] = lax.dot_general(
            results[i, j].reshape(tokens, UNIT),
            tokens_held[0],
            down,
            preferred_element_type=jnp.float32,
        ).astype(jnp.bfloat16)
        for kind in range(2):

            @pl.when((i == kind) & (j < blocks - 1))
            def _():
                out_copy(kind, kind, j, UNIT).start()

            @pl.when((i == kind) & (j == blocks - 1))
            def _():
                out_copy(kind, kind, j, last).start()

    def drain(kind):
        if blocks > 1:
            out_copy(kind, kind, blocks - 2, UNIT).wait()
        out_copy(kind, kind, blocks - 1, last).wait()

    def nth_chip(e):
        high, low = chips - 1 - e, e
        high = high - jnp.where(high <= chip, 1, 0)
        low = low + jnp.where(low >= chip, 1, 0)
        other = jnp.where(chip * 2 < chips, high, low)
        return jnp.where(e == chips - 1, chip, other)

    def pair(e):
        where = nth_chip(e)
        return pltpu.make_async_remote_copy(
            src_ref=spread.at[1 - core, where],
            dst_ref=pair_in.at[where],
            send_sem=pair_sem.at[0, where],
            recv_sem=pair_sem.at[1, where],
            device_id=(other_core, col),
            device_id_type=MESH,
        )

    def chip_copy(e):
        where = nth_chip(e)
        return pltpu.make_async_remote_copy(
            src_ref=spread.at[core, where],
            dst_ref=chip_in.at[chip],
            send_sem=chip_sem.at[0, where],
            recv_sem=chip_sem.at[1, chip],
            device_id=(where * 2 + core, col),
            device_id_type=MESH,
        )

    def chip_arrival(e):
        where = nth_chip(e)
        return pltpu.make_async_remote_copy(
            src_ref=spread.at[core, where],
            dst_ref=chip_in.at[where],
            send_sem=chip_sem.at[0, where],
            recv_sem=chip_sem.at[1, where],
            device_id=(where * 2 + core, col),
            device_id_type=MESH,
        )

    def place(owner):
        wanted = held_ref[:, pl.ds(pl.multiple_of(owner * slots, slots), slots)]
        ids = lax.broadcasted_iota(jnp.int32, (tokens, slots), 0)
        spread[lax.rem(owner, 2), lax.div(owner, 2)] = lax.dot_general(
            (ids == wanted).astype(jnp.bfloat16),
            weights[2, pl.ds(0, tokens), :],
            down,
            preferred_element_type=jnp.float32,
        ).astype(jnp.bfloat16)

    def combine(e):
        pair(e).wait_recv()
        where = nth_chip(e)
        spread[core, where] = (
            spread[core, where].astype(jnp.float32) + pair_in[where].astype(jnp.float32)
        ).astype(jnp.bfloat16)

    def hid_copy(j):
        return pltpu.make_async_copy(results.at[2, j], hid_ref.at[j], out_sem.at[2, j])

    def relay(k, carry):
        arrive(2, 2, k)
        start(3, 2, k)
        return carry

    def phase_back(j, carry):
        arrive(3, 0, j)
        arrive(3, 1, j)

        def term(n, c):
            i, a = lax.rem(n, 2), lax.div(n, 2)
            acc[half_rows(a), :] += lax.dot_general(
                results[i, j, a].reshape(2 * quarter, UNIT),
                weights[i, block_rows(j), :],
                plain,
                preferred_element_type=jnp.float32,
            )
            return c

        lax.fori_loop(0, 4, term, 0)

        @pl.when(j == blocks - 1)
        def _():
            weights[2, pl.ds(0, tokens), :] = acc[...].astype(jnp.bfloat16)

            def hand_over(n, c):
                e, mine = lax.div(n, 2), lax.rem(n, 2)
                side = jnp.where(mine == 1, core, 1 - core)
                place(nth_chip(e) * 2 + side)

                @pl.when(mine == 0)
                def _():
                    pair(e).start()

                @pl.when((mine == 1) & (e > 0))
                def _():
                    combine(e - 1)
                    chip_copy(e - 1).start()

                @pl.when((n > 0) & (n <= blocks))
                def _():
                    relay(n - 1, 0)

                return c

            lax.fori_loop(0, 2 * chips, hand_over, 0)
            if blocks > 2 * chips - 1:
                lax.fori_loop(2 * chips - 1, blocks, relay, 0)

        def both(i, c):
            emit(i, j)
            return c

        return lax.fori_loop(0, 2, both, carry)

    lax.fori_loop(0, blocks, phase_back, 0)
    combine(chips - 1)

    def phase_last(j, carry):
        arrive(3, 2, j)
        hid_copy(j).start()
        return carry

    lax.fori_loop(0, blocks, phase_last, 0)
    total = spread[core, chip].astype(jnp.float32)
    for e in range(chips - 1):
        chip_arrival(e).wait_recv()
        total = total + chip_in[nth_chip(e)].astype(jnp.float32)
    gi_ref[...] = total.astype(jnp.bfloat16)

    def phase_kept(j, carry):
        hid_copy(j).wait()
        return carry

    lax.fori_loop(0, blocks, phase_kept, 0)

    def phase_sent(j, carry):
        for step in range(4):
            for i in range(3):
                each_way(i, j, lambda way: copy(step, i, j, way).wait_send())
        return carry

    lax.fori_loop(0, blocks, phase_sent, 0)
    for e in range(chips):
        pair(e).wait_send()
    for e in range(chips - 1):
        chip_copy(e).wait_send()
    drain(0)
    drain(1)
    keep_grad.wait()


def finish_kernel(
    dims,
    gi_ref,
    gg_ref,
    gu_ref,
    hid_ref,
    pg_ref,
    gi_out,
    gg_out,
    gu_out,
    gd_out,
    low,
    whole,
    grads,
    hidden,
    down_grad,
    in_sem,
    out_sem,
    part_in,
    part_out,
    hid_sem,
    gd_sem,
):
    units, blocks, parts = dims
    rows = -(-units // (parts * 16)) * 16
    last = units - (blocks - 1) * UNIT
    pairs = []
    for i, (source, target) in enumerate(((gg_ref, gg_out), (gu_ref, gu_out))):
        for n in range(parts):
            where = pl.ds(n * rows, min(rows, units - n * rows))
            pairs.append(
                (
                    pltpu.make_async_copy(
                        source.at[where], whole.at[i, where], part_in.at[i, n]
                    ),
                    pltpu.make_async_copy(
                        whole.at[i, where], target.at[where], part_out.at[i, n]
                    ),
                )
            )
    bring_grads = pltpu.make_async_copy(pg_ref, grads, in_sem.at[0])
    bring_low = pltpu.make_async_copy(gi_ref, low, in_sem.at[1])
    put_low = pltpu.make_async_copy(low, gi_out, out_sem)
    bring = [
        pltpu.make_async_copy(hid_ref.at[j], hidden.at[j], hid_sem.at[j]) for j in range(blocks)
    ]
    bring_grads.start()
    bring[0].start()
    bring_low.start()
    for move, _ in pairs[:2]:
        move.start()
    for j in range(1, blocks):
        bring[j].start()
    for move, _ in pairs[2:]:
        move.start()
    bring_low.wait()
    put_low.start()
    bring_grads.wait()
    tokens = grads.shape[0]

    def put(j):
        where = pl.ds(j * UNIT, UNIT if j < blocks - 1 else last)
        return pltpu.make_async_copy(down_grad.at[where], gd_out.at[where], gd_sem.at[j])

    def block(j, carry):
        pltpu.make_async_copy(hid_ref.at[j], hidden.at[j], hid_sem.at[j]).wait()
        down_grad[pl.ds(pl.multiple_of(j * UNIT, UNIT), UNIT), :] = lax.dot_general(
            hidden[j].reshape(tokens, UNIT),
            grads[...],
            (((0,), (0,)), ((), ())),
            preferred_element_type=jnp.float32,
        ).astype(jnp.bfloat16)
        for k in range(blocks):

            @pl.when(j == k)
            def _():
                put(k).start()
                for move, out in pairs[len(pairs) * k // blocks : len(pairs) * (k + 1) // blocks]:
                    move.wait()
                    out.start()

        return carry

    lax.fori_loop(0, blocks, block, 0)
    for j in range(blocks):
        put(j).wait()
    for _, out in pairs:
        out.wait()
    put_low.wait()


def finish(grad_input, grad_gate, grad_up, hid, packed_grad):
    units, width = grad_gate.shape
    blocks, tokens = hid.shape[0], packed_grad.shape[0]
    low = jnp.bfloat16
    parts = 3
    any_space = pl.BlockSpec(memory_space=pltpu.HBM)
    whole = jax.ShapeDtypeStruct((units, width), low)
    return pl.pallas_call(
        functools.partial(finish_kernel, (units, blocks, parts)),
        out_shape=[jax.ShapeDtypeStruct(grad_input.shape, low), whole, whole, whole],
        in_specs=[any_space] * 5,
        out_specs=[any_space] * 4,
        scratch_shapes=[
            pltpu.VMEM(grad_input.shape, low),
            pltpu.VMEM((2, units, width), low),
            pltpu.VMEM((tokens, width), low),
            pltpu.VMEM(hid.shape, low),
            pltpu.VMEM((blocks * UNIT, width), low),
            pltpu.SemaphoreType.DMA((2,)),
            pltpu.SemaphoreType.DMA,
            pltpu.SemaphoreType.DMA((2, parts)),
            pltpu.SemaphoreType.DMA((2, parts)),
            pltpu.SemaphoreType.DMA((blocks,)),
            pltpu.SemaphoreType.DMA((blocks,)),
        ],
        compiler_params=pltpu.CompilerParams(vmem_limit_bytes=67_000_000),
        cost_estimate=pl.CostEstimate(
            flops=2 * tokens * width * units, bytes_accessed=14 * width * units, transcendentals=0
        ),
    )(grad_input, grad_gate, grad_up, hid, packed_grad)


def fused_layer(
    tokens, call_id, packed, cot_cols, weights, target, held_at, gate_weight, up_weight, down_weight
):
    units, width = down_weight.shape
    row_count = lax.axis_size("row")
    chips = row_count // 2
    slots = held_at.shape[1] // row_count
    blocks = -(-units // UNIT)
    quarter = tokens // 4
    low = jnp.bfloat16
    any_space = pl.BlockSpec(memory_space=pltpu.HBM)
    vmem = pl.BlockSpec(memory_space=pltpu.VMEM)
    whole = jax.ShapeDtypeStruct((units, width), low)
    done = pl.pallas_call(
        functools.partial(fused_kernel, (tokens, units, blocks)),
        out_shape=[
            jax.ShapeDtypeStruct((slots, width), low),
            whole,
            whole,
            jax.ShapeDtypeStruct((blocks, 2, 2, quarter, UNIT), low),
            jax.ShapeDtypeStruct((tokens, width), low),
        ],
        in_specs=[
            any_space,
            any_space,
            pl.BlockSpec(memory_space=pltpu.SMEM),
            vmem,
            vmem,
            any_space,
            any_space,
            any_space,
        ],
        out_specs=[vmem, any_space, any_space, any_space, any_space],
        scratch_shapes=[
            pltpu.VMEM((3, max(blocks * UNIT, tokens), width), low),
            pltpu.VMEM((2, tokens, width), low),
            pltpu.VMEM((max(row_count * cot_cols.shape[0], 4 * UNIT), width), low),
            pltpu.VMEM((3, blocks, 2, 2, quarter, UNIT), low),
            pltpu.VMEM((3, blocks, 2, quarter, UNIT), low),
            pltpu.VMEM((3, blocks, quarter, UNIT), low),
            pltpu.VMEM((3, blocks, 2, 2, quarter, UNIT), low),
            pltpu.VMEM((tokens, width), jnp.float32),
            pltpu.VMEM((2, chips, slots, width), low),
            pltpu.VMEM((chips, slots, width), low),
            pltpu.VMEM((chips, slots, width), low),
            pltpu.SemaphoreType.DMA((4, 3, blocks)),
            pltpu.SemaphoreType.DMA((4, 3, blocks)),
            pltpu.SemaphoreType.DMA((3, blocks)),
            pltpu.SemaphoreType.DMA((2,)),
            pltpu.SemaphoreType.DMA((3, row_count)),
            pltpu.SemaphoreType.DMA((row_count,)),
            pltpu.SemaphoreType.DMA((3, max(blocks, 2))),
            pltpu.SemaphoreType.DMA((2, chips)),
            pltpu.SemaphoreType.DMA((2, chips)),
        ],
        compiler_params=pltpu.CompilerParams(
            collective_id=call_id, has_side_effects=True, vmem_limit_bytes=67_000_000
        ),
        cost_estimate=pl.CostEstimate(
            flops=16 * tokens * width * units, bytes_accessed=12 * width * units, transcendentals=0
        ),
    )(
        packed,
        cot_cols,
        weights,
        target,
        held_at,
        gate_weight.T,
        up_weight.T,
        down_weight,
    )
    grad_input, grad_gate, grad_up, grad_down = finish(*done)
    return grad_input, grad_gate.T, grad_up.T, grad_down


def column_sum(a, bs):
    dims = (((1,), (1,)), ((), ()))
    return [
        lax.psum(
            lax.dot_general(a, b, dims, preferred_element_type=jnp.float32).astype(jnp.bfloat16),
            "col",
        )
        for b in bs
    ]


def per_device(
    roll_hidden,
    roll_cotangent,
    lengths,
    owners,
    prompts,
    rewards,
    gate_weight,
    up_weight,
    down_weight,
):
    row_count = lax.axis_size("row")
    col_count = lax.axis_size("col")
    total_tokens = row_count * CAPR
    count_prompts = row_count * col_count // 8
    slot_count = roll_hidden.shape[0]
    width = roll_hidden.shape[1] // col_count
    local = jnp.stack(
        [
            lengths.astype(jnp.float32),
            owners.astype(jnp.float32),
            prompts.astype(jnp.float32),
            rewards,
        ],
        axis=1,
    )
    fused = col_count == 4 and row_count % 2 == 0 and row_count >= 4
    if fused:
        sizes = [total_tokens * part // 16 for part in SIZES]
        choice, packed, cot_cols, spots, held_at, weights = gather_rows(
            local, roll_hidden, roll_cotangent, total_tokens, sizes
        )
        return lax.switch(
            choice[0, 0],
            [
                functools.partial(fused_layer, size, 3 + i)
                for i, size in enumerate(sizes + [total_tokens])
            ],
            packed,
            cot_cols,
            weights,
            spots,
            held_at,
            gate_weight,
            up_weight,
            down_weight,
        )
    table = gather_table(local)
    all_lengths = table[:, 0].astype(jnp.int32)
    all_owners = table[:, 1].astype(jnp.int32)
    all_prompts = table[:, 2].astype(jnp.int32)
    weights = row_weights(all_lengths, all_prompts, table[:, 3], count_prompts)
    offsets = row_offsets(all_lengths, all_owners)
    starts = jnp.cumsum(all_lengths) - all_lengths
    live_total = jnp.sum(all_lengths)
    firsts = all_owners * CAPR + offsets
    places = jnp.arange(total_tokens, dtype=jnp.int32)[:, None]
    inside = (places >= firsts[None, :]) & (places < (firsts + all_lengths)[None, :])
    held_at = jnp.sum(jnp.where(inside, places + (starts - firsts + 1)[None, :], 0), 1) - 1

    slots = jnp.arange(slot_count, dtype=jnp.int32)
    target = jnp.where(
        slots[None, :] < all_lengths[:, None], starts[:, None] + slots[None, :], total_tokens
    ).reshape(-1)
    slot_weights = jnp.repeat(weights, slot_count)
    def to_cols(rolled):
        blocks = rolled.reshape(slot_count, col_count, width)
        return lax.all_to_all(blocks, "col", split_axis=1, concat_axis=0, tiled=True).reshape(
            col_count * slot_count, width
        )

    hidden_cols, roll_cotangent = lax.optimization_barrier((to_cols(roll_hidden), roll_cotangent))
    hidden_all = lax.all_gather(hidden_cols, "row", axis=0, tiled=True)
    operands = (
        hidden_all,
        to_cols(roll_cotangent),
        target,
        slot_weights,
        held_at,
        gate_weight,
        up_weight,
        down_weight,
    )
    return layer(total_tokens, *operands)


def layer(
    tokens,
    hidden_all,
    cotangent_cols,
    target,
    slot_weights,
    held_at,
    gate_weight,
    up_weight,
    down_weight,
):
    ids = jnp.arange(tokens, dtype=jnp.int32)
    pick = (ids[:, None] == target[None, :]).astype(jnp.bfloat16)
    spread_out = (held_at[:, None] == ids[None, :]).astype(jnp.bfloat16)

    def move(onehot, every):
        return jnp.dot(onehot, every, preferred_element_type=jnp.float32).astype(jnp.bfloat16)

    cotangent_all = lax.all_gather(cotangent_cols, "row", axis=0, tiled=True)
    packed = move(pick, hidden_all)
    gate, upval = column_sum(packed, (gate_weight.T, up_weight.T))
    slot_weights, gate, upval = lax.optimization_barrier((slot_weights, gate, upval))
    packed_grad = move(
        pick, (cotangent_all.astype(jnp.float32) * slot_weights[:, None]).astype(jnp.bfloat16)
    )
    (grad_hidden,) = column_sum(packed_grad, (down_weight,))
    gate, upval, grad_hidden = (v.astype(jnp.float32) for v in (gate, upval, grad_hidden))
    sig = jax.nn.sigmoid(gate)
    silu = gate * sig
    hidden = (silu * upval).astype(jnp.bfloat16)
    contract_cols = (((1,), (1,)), ((), ()))
    grad_gate_act = (grad_hidden * upval * sig * (1.0 + gate * (1.0 - sig))).astype(jnp.bfloat16)
    grad_up_act = (grad_hidden * silu).astype(jnp.bfloat16)
    contract_rows = (((0,), (0,)), ((), ()))
    grad_down = lax.dot_general(
        hidden, packed_grad, contract_rows, preferred_element_type=jnp.float32
    ).astype(jnp.bfloat16)
    grad_gate = lax.dot_general(
        packed, grad_gate_act, contract_rows, preferred_element_type=jnp.float32
    ).astype(jnp.bfloat16)
    grad_up = lax.dot_general(
        packed, grad_up_act, contract_rows, preferred_element_type=jnp.float32
    ).astype(jnp.bfloat16)
    term = lax.dot_general(
        grad_gate_act, gate_weight, contract_cols, preferred_element_type=jnp.float32
    )
    term = (
        term
        + lax.dot_general(
            grad_up_act, up_weight, contract_cols, preferred_element_type=jnp.float32
        )
    ).astype(jnp.bfloat16)
    grad_input = lax.psum_scatter(
        move(spread_out, term), "row", scatter_dimension=0, tiled=True
    )
    return (grad_input, grad_gate, grad_up, grad_down)


def solution(mesh):
    return jax.shard_map(
        per_device,
        mesh=mesh,
        in_specs=(
            P(("row", "col"), None),
            P(("row", "col"), None),
            P(("row", "col")),
            P(("row", "col")),
            P(("row", "col")),
            P(("row", "col")),
            P("col", "row"),
            P("col", "row"),
            P("row", "col"),
        ),
        out_specs=(P("row", "col"), P("col", "row"), P("col", "row"), P("row", "col")),
        check_vma=False,
    )
```
